32 devices in a mesh: tm: 4 (over y, core), scen: 8 (over z, x).
Axes of the slice: x: 2, y: 2, z: 4, core: 2. Of those that a mesh axis runs over, the one named last changes fastest.
Arguments:
- prior_dispatch: float32 [600, 8192], P(None, ('tm', 'scen')), may hold values from 0 to 1
- prior_commitment: float32 [600, 8192], P(None, ('tm', 'scen')), may hold values from 0 to 1
- prior_consensus: float32 [600, 32], P(None, 'tm'), may hold values from 0 to 1
- prior_multiplier: float32 [600, 8192], P(None, ('tm', 'scen')), may hold values from -2 to 2
- flow_factors: bfloat16 [2560, 2000], P('scen'), may hold values from -0.25 to 0.25
- unit_buses: int32 [600], replicated, may hold values from 0 to 1999
- wind_buses: int32 [128], replicated, may hold values from 0 to 1999
- wind_output: bfloat16 [128, 8192], P(None, ('tm', 'scen')), may hold values from 0 to 1
- demand: float32 [32], P('tm'), may hold values from 180 to 300
- load_flows: bfloat16 [2560, 32], P('scen', 'tm'), may hold values from -6 to 6
- line_limits: bfloat16 [2560], P('scen'), may hold values from 0.29882812 to 3
- unit_table: float32 [5, 600], replicated, may hold values from 0.05 to 2, as said below
Outputs:
- dispatch: float32 [600, 8192], P(None, ('tm', 'scen'))
- commitment: float32 [600, 8192], P(None, ('tm', 'scen'))
- consensus: float32 [600, 32], P(None, 'tm')
- multiplier: float32 [600, 8192], P(None, ('tm', 'scen'))
The draws below stay inside these ranges and needn't reach their ends.
Inputs may be any that keep to these rules, and one draw needn't show every extreme that they name: `unit_table`: rows 0 and 4 lie in 0.1 to 1, row 1 in 0.05 to 0.5, row 2 in 0.5 to 2, row 3 in 0.05 to 0.5.
All inputs are finite; a program needn't handle non-finite values.
Results may differ from the reference program's by a relative error of at most 0.0017.
Values may be sent and summed in bfloat16 or wider, within the bound.
A program may use at most 64 MiB of HBM per device.

```python
import math
import jax
import jax.numpy as jnp
from jax import lax

UNITS = 600
BUSES = 2000
LINES = 2560
FARMS = 128
PASSES = 3
H_DEV = 8
S_DEV = 32
HOURS = 32
SCENARIOS = 256
COLS = 8192
N_TM = 4
N_SCEN = 8


def draw_unit_table(key, part):
    keys = jax.random.split(jax.random.fold_in(key, 11), 5)
    linear = jax.random.uniform(keys[0], (UNITS,), jnp.float32, 0.1, 1.0)
    quadratic = jnp.exp(jax.random.uniform(keys[1], (UNITS,), jnp.float32, math.log(0.05), math.log(0.5)))
    capacity = jnp.exp(jax.random.uniform(keys[2], (UNITS,), jnp.float32, math.log(0.5), math.log(2.0)))
    ramp_limit = jnp.exp(jax.random.uniform(keys[3], (UNITS,), jnp.float32, math.log(0.05), math.log(0.5)))
    noload = jax.random.uniform(keys[4], (UNITS,), jnp.float32, 0.1, 1.0)
    return jnp.stack([linear, quadratic, capacity, ramp_limit, noload], axis=0)


def draw_prior_multiplier(key, part):
    keys = jax.random.split(jax.random.fold_in(key, 23), 2)
    offset = jax.random.uniform(keys[0], (UNITS, 1), jnp.float32, -1.5, 1.5)
    noise = jax.random.uniform(keys[1], (UNITS, COLS), jnp.float32, -0.5, 0.5)
    return offset + noise


def place_ends(values, own_key, low, largest):
    place = [jax.random.randint(jax.random.fold_in(own_key, axis), (), 0, length) for axis, length in enumerate(values.shape)]
    main_axis = values.shape.index(max(values.shape))
    beside = place[:main_axis] + [(place[main_axis] + 1) % values.shape[main_axis]] + place[main_axis + 1:]
    return values.at[tuple(place)].set(low).at[tuple(beside)].set(largest)


def block_scale(key, extent, cuts, least, largest):
    loudness, own = 1.0, jax.random.fold_in(key, 6)
    for dim, shards_of in cuts:
        steps = jnp.exp(jax.random.uniform(jax.random.fold_in(own, dim), (shards_of,), jnp.float32, least / len(cuts), largest / len(cuts)))
        loudness = loudness * jnp.repeat(steps, extent[dim] // shards_of).reshape([-1 if axis == dim else 1 for axis in range(len(extent))])
    return loudness


def gaussian(rng, shape, deviation, limit, shards=(), held_as=jnp.bfloat16):
    drawn = jax.random.normal(rng, shape, jnp.float32) * deviation
    if len(shards) > 0:
        drawn = block_scale(rng, shape, shards, -0.22, 0.18) * drawn
    return jnp.clip(drawn, min=-limit, max=limit).astype(held_as)


def setup_inputs(seed: int = 0) -> dict:
    streams_of = jax.random.split(jax.random.key(seed), 13)
    prior_dispatch = jnp.clip(1.0 * jax.random.uniform(streams_of[0], (UNITS, COLS), jnp.float32) ** block_scale(streams_of[0], (UNITS, COLS), ((1, 32),), -0.2, 0.2), 0.0, 1.0)
    prior_commitment = jnp.clip(1.0 * jax.random.uniform(streams_of[1], (UNITS, COLS), jnp.float32) ** block_scale(streams_of[1], (UNITS, COLS), ((1, 32),), -0.2, 0.2), 0.0, 1.0)
    prior_consensus = jnp.clip(1.0 * jax.random.uniform(streams_of[2], (UNITS, HOURS), jnp.float32) ** block_scale(streams_of[2], (UNITS, HOURS), ((1, 4),), -0.2, 0.2), 0.0, 1.0)
    prior_multiplier = draw_prior_multiplier(jax.random.fold_in(streams_of[12], 71), 0)
    flow_factors = gaussian(streams_of[4], (LINES, BUSES), UNITS ** -0.5, 0.25, ((0, 8),))
    unit_buses = place_ends(jax.random.randint(streams_of[5], (UNITS,), 0, BUSES), jax.random.fold_in(streams_of[5], 1), 0, BUSES - 1).astype(jnp.int32)
    wind_buses = place_ends(jax.random.randint(streams_of[6], (FARMS,), 0, BUSES), jax.random.fold_in(streams_of[6], 1), 0, BUSES - 1).astype(jnp.int32)
    wind_output = jnp.clip(1.0 * jax.random.uniform(streams_of[7], (FARMS, COLS), jnp.float32) ** block_scale(streams_of[7], (FARMS, COLS), ((1, 32),), -0.2, 0.2), 0.0, 1.0).astype(jnp.bfloat16)
    demand = jnp.clip(180.0 + 120.0 * jax.random.uniform(streams_of[8], (HOURS,), jnp.float32) ** block_scale(streams_of[8], (HOURS,), ((0, 4),), -0.2, 0.2), 180.0, 300.0)
    load_flows = gaussian(streams_of[9], (LINES, HOURS), 1.0, 6.0, ((0, 8), (1, 4)))
    line_limits = jnp.clip(jnp.exp(math.log(3.0) - 2.306499 * jax.random.uniform(streams_of[10], (LINES,), jnp.float32) ** block_scale(streams_of[10], (LINES,), ((0, 8),), -0.2, 0.2)), 0.29882812, 3.0).astype(jnp.bfloat16)
    unit_table = draw_unit_table(jax.random.fold_in(streams_of[12], 71), 0)
    return {"prior_dispatch": prior_dispatch, "prior_commitment": prior_commitment, "prior_consensus": prior_consensus, "prior_multiplier": prior_multiplier, "flow_factors": flow_factors, "unit_buses": unit_buses, "wind_buses": wind_buses, "wind_output": wind_output, "demand": demand, "load_flows": load_flows, "line_limits": line_limits, "unit_table": unit_table}


flow_weight = 0.5
ramp_weight = 1.0
balance_weight = 0.004
short_weight = 2.0
penalty = 1.0
step_power = 0.2
step_commit = 0.3


def to_grid(array):
    rows = array.shape[0]
    array = array.reshape(rows, N_TM, N_SCEN, H_DEV, S_DEV).transpose(0, 1, 3, 2, 4)
    return array.reshape(rows, HOURS, SCENARIOS)


def from_grid(array):
    rows = array.shape[0]
    array = array.reshape(rows, N_TM, H_DEV, N_SCEN, S_DEV).transpose(0, 1, 3, 2, 4)
    return array.reshape(rows, COLS)


def reference(prior_dispatch, prior_commitment, prior_consensus, prior_multiplier, flow_factors, unit_buses, wind_buses, wind_output, demand, load_flows, line_limits, unit_table):
    linear = unit_table[0][:, None, None]
    quadratic = unit_table[1][:, None, None]
    capacity = unit_table[2][:, None, None]
    ramp_limit = unit_table[3][:, None, None]
    noload = unit_table[4][:, None, None]
    factors = jnp.concatenate([flow_factors[:, unit_buses], flow_factors[:, wind_buses]], axis=1)
    gen_factors = factors[:, :UNITS]
    power = to_grid(prior_dispatch)
    commit = to_grid(prior_commitment)
    multiplier = to_grid(prior_multiplier)
    wind = to_grid(wind_output)
    wind_hours = wind.transpose(1, 0, 2)
    wind_total = jnp.sum(wind.astype(jnp.float32), axis=0)
    target = prior_consensus[:, :, None]
    hourly = load_flows.astype(jnp.float32).T
    bounds = line_limits.astype(jnp.float32)[:, None]

    def per_hour(items):
        power_hour, wind_hour, load_hour = items
        extended = jnp.concatenate([power_hour, wind_hour], axis=0)
        flows = jnp.dot(factors, extended, preferred_element_type=jnp.float32) - load_hour[:, None]
        excess = flows - jnp.clip(flows, -bounds, bounds)
        return jnp.dot(gen_factors.T, excess.astype(jnp.bfloat16), preferred_element_type=jnp.float32)

    for number in range(PASSES):
        rounded = power.astype(jnp.bfloat16).transpose(1, 0, 2)
        back = lax.map(per_hour, (rounded, wind_hours, hourly)).transpose(1, 0, 2)
        previous = jnp.concatenate([power[:, :1], power[:, :-1]], axis=1)
        rate = power - previous
        over = rate - jnp.clip(rate, -ramp_limit, ramp_limit)
        following = jnp.concatenate([over[:, 1:], jnp.zeros_like(over[:, :1])], axis=1)
        ramp_term = over - following
        balance = jnp.sum(power, axis=0) + wind_total - demand[:, None]
        short = jnp.maximum(power - capacity * commit, 0.0)
        grad_power = linear + 2.0 * quadratic * power + flow_weight * back + ramp_weight * ramp_term + balance_weight * balance + short_weight * short
        grad_commit = noload - short_weight * capacity * short + multiplier + penalty * (commit - target)
        power = jnp.clip(power - step_power * grad_power, 0.0, capacity)
        commit = jnp.clip(commit - step_commit * grad_commit, 0.0, 1.0)
    consensus = jnp.clip(jnp.sum(commit + multiplier / penalty, axis=2) / SCENARIOS, 0.0, 1.0)
    updated = multiplier + penalty * (commit - consensus[:, :, None])
    return from_grid(power), from_grid(commit), consensus, from_grid(updated)
```

```python
import functools

import jax
import jax.numpy as jnp
from jax import lax
from jax.experimental import pallas as pl
from jax.experimental.pallas import tpu as pltpu
from jax.sharding import PartitionSpec as P

PASSES = 3
H_DEV = 8
MESH = pl.DeviceIdType.MESH

flow_weight = 0.5
ramp_weight = 1.0
balance_weight = 0.004
short_weight = 2.0
penalty = 1.0
step_power = 0.2
step_commit = 0.3


def kernel(n_tm, n_scen, units, sel_ref, tab_ref, pd_ref, pc_ref, cons_ref, mu_ref, wind_ref, need_ref, ut_ref,
           power_out, commit_out, cons_out, upd_out,
           fac, fact, load, bound, exc, pw, cm, mult, target, ext, backs, bef, aft,
           tabs, esend, erecv, psend, precv, total_row,
           recv_sem, send_sem, tsend, trecv, esem_s, esem_r, psem_s, psem_r):
    rows = sel_ref.shape[0]
    quarter = rows // 4
    up = pw.shape[0]
    cols = pw.shape[1]
    block = cols // H_DEV
    chunk = 2 * rows
    n_z = n_scen // 2
    f32, bf16 = jnp.float32, jnp.bfloat16
    tm = lax.axis_index("tm")
    scen = lax.axis_index("scen")
    y, c = tm // 2, tm % 2
    z, x = scen // 2, scen % 2
    oy = 1 - y
    oc = 1 - c
    ox = 1 - x
    mine = y * 2 + c
    other = oy * 2 + c
    dev_x = (tm, z * 2 + ox)
    dev_y = (oy * 2 + c, scen)
    dev_c = (y * 2 + oc, scen)
    dev_dn = (tm, scen - 2)
    dev_up = (tm, scen + 2)

    def piece(zz, xx, q):
        return (zz * 2 + xx) * 4 + q

    def at(p):
        return fac.at[pl.ds(pl.multiple_of(p * quarter, 16), quarter), :]

    def own(q):
        return sel_ref.at[pl.ds(pl.multiple_of(q * quarter, 16), quarter), :]

    def copy(src, p, slot, dev):
        return pltpu.make_async_remote_copy(
            src_ref=src, dst_ref=at(p), send_sem=send_sem.at[slot, p], recv_sem=recv_sem.at[p],
            device_id=dev, device_id_type=MESH)

    def pass_on(p, slot, dev):
        copy(at(p), p, slot, dev).start()

    def arrived(p):
        copy(at(p), p, 0, dev_x).wait_recv()

    def table_copy(k):
        peer = lax.rem(scen + k, n_scen)
        return pltpu.make_async_remote_copy(
            src_ref=tab_ref, dst_ref=tabs.at[scen], send_sem=tsend.at[k], recv_sem=trecv.at[scen],
            device_id=(tm, peer), device_id_type=MESH)

    barrier = pltpu.get_barrier_semaphore()
    for k in range(1, n_scen):
        pl.semaphore_signal(barrier, inc=1, device_id=(tm, lax.rem(scen + k, n_scen)), device_id_type=MESH)
    for k in range(1, n_tm):
        pl.semaphore_signal(barrier, inc=1, device_id=(lax.rem(tm + k, n_tm), scen), device_id_type=MESH)
    pl.semaphore_wait(barrier, n_scen - 1 + n_tm - 1)

    p_own = piece(z, x, mine)
    p_own2 = piece(z, x, other)

    @pl.when(z > 0)
    def _():
        copy(own(mine), p_own, 0, dev_dn).start()

    @pl.when(z < n_z - 1)
    def _():
        copy(own(mine), p_own, 1, dev_up).start()

    copy(own(mine), p_own, 2, dev_x).start()
    copy(own(other), p_own2, 2, dev_x).start()
    for k in range(1, n_scen):
        table_copy(k).start()

    def edges_of(tile_last, tile_first):
        lane = lax.broadcasted_iota(jnp.int32, (up // 4, 128), 1)
        last = jnp.zeros((up // 4, 128), f32)
        first = jnp.zeros((up // 4, 128), f32)
        for g in range(4):
            inside = (lane >= 32 * g) & (lane < 32 * g + 32)
            a = tile_last[g * (up // 4):(g + 1) * (up // 4), :]
            b = tile_first[g * (up // 4):(g + 1) * (up // 4), :]
            sa = (32 * g - 96) % 128
            sb = (32 * g) % 128
            a = pltpu.roll(a, sa, 1) if sa else a
            b = pltpu.roll(b, sb, 1) if sb else b
            last = jnp.where(inside, a, last)
            first = jnp.where(inside, b, first)
        return last, first

    def edge_copy(number, way):
        dev = (tm + 1, scen) if way == 0 else (tm - 1, scen)
        return pltpu.make_async_remote_copy(
            src_ref=esend.at[number, way], dst_ref=erecv.at[number, way],
            send_sem=esem_s.at[number, way], recv_sem=esem_r.at[number, way],
            device_id=dev, device_id_type=MESH)

    def send_edges(number):
        @pl.when(tm < n_tm - 1)
        def _():
            edge_copy(number, 0).start()

        @pl.when(tm > 0)
        def _():
            edge_copy(number, 1).start()

    def store_edges(number):
        last, first = edges_of(pw[:, cols - 128:], pw[:, :128])
        esend[number, 0] = last
        esend[number, 1] = first

    zero_tail = jnp.zeros((up - units, cols), f32)
    pw[:units, :] = pd_ref[...]
    pw[units:, :] = zero_tail
    store_edges(0)
    cm[:units, :] = pc_ref[...]
    cm[units:, :] = zero_tail
    mult[:units, :] = mu_ref[...]
    mult[units:, :] = zero_tail
    hour_row = lax.broadcasted_iota(jnp.int32, (H_DEV, cols), 0)
    hour_col = lax.broadcasted_iota(jnp.int32, (H_DEV, cols), 1)
    hour_of = ((hour_col >= hour_row * block) & (hour_col < hour_row * block + block)).astype(f32)
    target[...] = jnp.dot(cons_ref[...], hour_of, preferred_element_type=f32, precision=lax.Precision.HIGHEST)
    fac[pl.ds(pl.multiple_of(scen * rows, 16), rows), :] = sel_ref[...]
    tabs[scen] = tab_ref[...]
    ext[:up, :] = pw[...].astype(bf16)
    ext[up:, :] = wind_ref[...]
    total_row[...] = jnp.sum(wind_ref[...].astype(f32), axis=0, keepdims=True) - need_ref[...]
    send_edges(0)

    def along_z(k):
        for down in (True, False):
            zz = z - k if down else z + k
            ok = zz >= 0 if down else zz < n_z

            @pl.when(ok)
            def _():
                p = piece(zz, x, mine)
                arrived(p)
                if down:
                    @pl.when(z < n_z - 1)
                    def _():
                        pass_on(p, 1, dev_up)
                else:
                    @pl.when(z > 0)
                    def _():
                        pass_on(p, 0, dev_dn)
                pass_on(p, 2, dev_x)
                pass_on(p, 3, dev_y)
                pass_on(p, 4, dev_c)

    def both(k, f):
        @pl.when(z - k >= 0)
        def _():
            f(z - k)

        @pl.when(z + k < n_z)
        def _():
            f(z + k)

    def across_x(zz):
        p = piece(zz, ox, mine)
        arrived(p)
        pass_on(p, 3, dev_y)
        pass_on(p, 4, dev_c)

    def from_y_same(zz):
        p = piece(zz, x, other)
        arrived(p)
        pass_on(p, 4, dev_c)

    def from_y_cross(zz):
        p = piece(zz, ox, other)
        arrived(p)
        pass_on(p, 4, dev_c)

    def own_plane_x():
        for q in (mine, other):
            p = piece(z, ox, q)
            arrived(p)
            pass_on(p, 4, dev_c)

    along_z(1)
    own_plane_x()
    for k in range(2, n_z + 1):
        if k < n_z:
            along_z(k)
        both(k - 1, across_x)
        both(k - 1, from_y_same)
        if k > 2:
            both(k - 2, from_y_cross)
    both(n_z - 1, from_y_cross)

    def from_core(zz):
        for xx in range(2):
            for yy in range(2):
                arrived(piece(zz, xx, yy * 2 + oc))

    for q in (oc, 2 + oc):
        arrived(piece(z, ox, q))
    for k in range(1, n_z):
        both(k, from_core)
    for k in range(1, n_scen):
        src = lax.rem(scen + k, n_scen)
        pltpu.make_async_remote_copy(
            src_ref=tab_ref, dst_ref=tabs.at[src], send_sem=tsend.at[k], recv_sem=trecv.at[src],
            device_id=dev_x, device_id_type=MESH).wait_recv()

    spread_row = lax.broadcasted_iota(jnp.int32, (16, cols), 0)
    spread_col = lax.broadcasted_iota(jnp.int32, (16, cols), 1)
    load_of = ((spread_col >= spread_row * block) & (spread_col < spread_row * block + block)).astype(bf16)
    limit_of = (spread_row == H_DEV).astype(bf16)
    lines_first = (((0,), (0,)), ((), ()))

    def prepare(s, carry):
        table = tabs[s]
        at_rows = pl.ds(pl.multiple_of(s * rows, 16), rows)
        load[at_rows, :] = lax.dot_general(table, load_of, lines_first, preferred_element_type=f32)[:rows]
        bound[at_rows, :] = lax.dot_general(table, limit_of, lines_first, preferred_element_type=f32)[:rows]
        return carry

    lax.fori_loop(0, n_scen, prepare, 0)

    def flip(k, carry):
        at_rows = pl.ds(pl.multiple_of(k * chunk, 128), chunk)
        fact[:, at_rows] = fac[at_rows, :up].T
        return carry

    lax.fori_loop(0, n_z, flip, 0)

    tile = 32
    lane = lax.broadcasted_iota(jnp.int32, (tile, cols), 1)
    for number in range(PASSES):
        if number > 0:
            send_edges(number)
        backs[...] = jnp.zeros((up, cols), f32)

        def fold(k, carry):
            at_rows = pl.ds(pl.multiple_of(k * chunk, 128), chunk)
            flows = jnp.dot(fac[at_rows, :], ext[...], preferred_element_type=f32) - load[at_rows, :]
            lim = bound[at_rows, :]
            exc[...] = (flows - jnp.clip(flows, -lim, lim)).astype(bf16)
            backs[...] += jnp.dot(fact[:, at_rows], exc[...], preferred_element_type=f32)
            return carry

        lax.fori_loop(0, n_z, fold, 0)

        @pl.when(tm > 0)
        def _():
            edge_copy(number, 0).wait_recv()
            for g in range(4):
                e = erecv[number, 0]
                s = (-32 * g) % 128
                bef[g * (up // 4):(g + 1) * (up // 4), :] = pltpu.roll(e, s, 1) if s else e

        @pl.when(tm == 0)
        def _():
            bef[...] = pw[:, :128]

        @pl.when(tm < n_tm - 1)
        def _():
            edge_copy(number, 1).wait_recv()
            for g in range(4):
                e = erecv[number, 1]
                s = (96 - 32 * g) % 128
                aft[g * (up // 4):(g + 1) * (up // 4), :] = pltpu.roll(e, s, 1) if s else e

        @pl.when(tm == n_tm - 1)
        def _():
            aft[...] = pw[:, cols - 128:]

        balance = jnp.sum(pw[...], axis=0, keepdims=True) + total_row[...]
        balance_part = balance_weight * balance

        def update(i, carry):
            r = pl.ds(pl.multiple_of(i * tile, tile), tile)
            power = pw[r, :]
            commit = cm[r, :]
            linear = ut_ref[r, 0:1]
            quadratic = ut_ref[r, 1:2]
            capacity = ut_ref[r, 2:3]
            ramp_limit = ut_ref[r, 3:4]
            noload = ut_ref[r, 4:5]
            b = bef[r, :]
            a = aft[r, :]
            previous = jnp.where(lane < block, jnp.concatenate([b] * (cols // 128), axis=1), pltpu.roll(power, block, 1))
            nxt = jnp.where(lane >= cols - block, jnp.concatenate([a] * (cols // 128), axis=1), pltpu.roll(power, cols - block, 1))
            rate = power - previous
            over = rate - jnp.clip(rate, -ramp_limit, ramp_limit)
            coming = nxt - power
            following = coming - jnp.clip(coming, -ramp_limit, ramp_limit)
            ramp_term = over - following
            short = jnp.maximum(power - capacity * commit, 0.0)
            grad_power = (linear + 2.0 * quadratic * power + flow_weight * backs[r, :] + ramp_weight * ramp_term
                          + balance_part + short_weight * short)
            grad_commit = noload - short_weight * capacity * short + mult[r, :] + penalty * (commit - target[r, :])
            new_power = jnp.clip(power - step_power * grad_power, 0.0, capacity)
            pw[r, :] = new_power
            cm[r, :] = jnp.clip(commit - step_commit * grad_commit, 0.0, 1.0)
            ext[r, :] = new_power.astype(bf16)
            return carry

        lax.fori_loop(0, up // tile, update, 0)
        if number < PASSES - 1:
            store_edges(number + 1)

    psend[...] = lax.dot_general(hour_of, cm[...] + mult[...] / penalty, (((1,), (1,)), ((), ())),
                                 preferred_element_type=f32, precision=lax.Precision.HIGHEST)
    power_out[...] = pw[:units, :]
    commit_out[...] = cm[:units, :]

    def sum_copy(k):
        return pltpu.make_async_remote_copy(
            src_ref=psend, dst_ref=precv.at[scen], send_sem=psem_s.at[k], recv_sem=psem_r.at[scen],
            device_id=(tm, lax.rem(scen + k, n_scen)), device_id_type=MESH)

    for k in range(1, n_scen):
        sum_copy(k).start()
    precv[scen] = psend[...]
    for k in range(1, n_scen):
        src = lax.rem(scen + k, n_scen)
        pltpu.make_async_remote_copy(
            src_ref=psend, dst_ref=precv.at[src], send_sem=psem_s.at[k], recv_sem=psem_r.at[src],
            device_id=dev_x, device_id_type=MESH).wait_recv()
    totals = precv[0]
    for k in range(1, n_scen):
        totals = totals + precv[k]
    consensus = jnp.clip(totals / (block * n_scen), 0.0, 1.0)
    flipped = consensus.T
    cons_out[...] = flipped[:units, :]
    wide = jnp.dot(flipped, hour_of, preferred_element_type=f32, precision=lax.Precision.HIGHEST)
    upd_out[...] = (mult[...] + penalty * (cm[...] - wide))[:units, :]

    @pl.when(z > 0)
    def _():
        copy(own(mine), p_own, 0, dev_dn).wait_send()

    @pl.when(z < n_z - 1)
    def _():
        copy(own(mine), p_own, 1, dev_up).wait_send()

    copy(own(mine), p_own, 2, dev_x).wait_send()
    copy(own(other), p_own2, 2, dev_x).wait_send()

    def left(p, slot, dev):
        copy(at(p), p, slot, dev).wait_send()

    for k in range(1, n_z):
        for down in (True, False):
            zz = z - k if down else z + k

            @pl.when(zz >= 0 if down else zz < n_z)
            def _():
                p = piece(zz, x, mine)
                if down:
                    @pl.when(z < n_z - 1)
                    def _():
                        left(p, 1, dev_up)
                else:
                    @pl.when(z > 0)
                    def _():
                        left(p, 0, dev_dn)
                left(p, 2, dev_x)
                left(p, 3, dev_y)
                left(p, 4, dev_c)
                p = piece(zz, ox, mine)
                left(p, 3, dev_y)
                left(p, 4, dev_c)
                left(piece(zz, x, other), 4, dev_c)
                left(piece(zz, ox, other), 4, dev_c)
    for q in (mine, other):
        left(piece(z, ox, q), 4, dev_c)
    for k in range(1, n_scen):
        table_copy(k).wait_send()
        sum_copy(k).wait_send()
    for number in range(PASSES):
        @pl.when(tm < n_tm - 1)
        def _():
            edge_copy(number, 0).wait_send()

        @pl.when(tm > 0)
        def _():
            edge_copy(number, 1).wait_send()


def selection(unit_buses, wind_buses, buses, up, dtype):
    units = unit_buses.shape[0]
    wanted = jnp.concatenate([unit_buses, jnp.full((up - units,), -1, unit_buses.dtype), wind_buses])
    return (lax.broadcasted_iota(jnp.int32, (buses, wanted.shape[0]), 0) == wanted[None, :]).astype(dtype)


def fused(n_tm, n_scen, prior_dispatch, prior_commitment, prior_consensus, prior_multiplier, flow_factors,
          unit_buses, wind_buses, wind_output, demand, load_flows, line_limits, unit_table):
    units, cols = prior_dispatch.shape
    rows, buses = flow_factors.shape
    farms = wind_output.shape[0]
    up = -(-units // 128) * 128
    f32, bf16 = jnp.float32, jnp.bfloat16
    sel = jnp.dot(flow_factors, selection(unit_buses, wind_buses, buses, up, bf16), preferred_element_type=f32).astype(bf16)
    lanes = -(-rows // 128) * 128
    table = jnp.concatenate([load_flows.T, line_limits[None, :]], axis=0)
    table = jnp.pad(table, ((0, 16 - table.shape[0]), (0, lanes - rows)))
    cons = jnp.pad(prior_consensus, ((0, up - units), (0, 0)))
    ut = jnp.pad(unit_table.T, ((0, up - units), (0, 0)))
    need = jnp.repeat(demand, cols // H_DEV)[None, :]
    lines = rows * n_scen
    chunk = 2 * rows
    wide = up + farms
    vm = pl.BlockSpec(memory_space=pltpu.VMEM)
    dma = pltpu.SemaphoreType.DMA
    return pl.pallas_call(
        functools.partial(kernel, n_tm, n_scen, units),
        name="window",
        out_shape=(
            jax.ShapeDtypeStruct((units, cols), f32),
            jax.ShapeDtypeStruct((units, cols), f32),
            jax.ShapeDtypeStruct((units, H_DEV), f32),
            jax.ShapeDtypeStruct((units, cols), f32),
        ),
        in_specs=[vm] * 9,
        out_specs=(vm,) * 4,
        scratch_shapes=[
            pltpu.VMEM((lines, wide), bf16),
            pltpu.VMEM((up, lines), bf16),
            pltpu.VMEM((lines, cols), f32),
            pltpu.VMEM((lines, cols), f32),
            pltpu.VMEM((chunk, cols), bf16),
            pltpu.VMEM((up, cols), f32),
            pltpu.VMEM((up, cols), f32),
            pltpu.VMEM((up, cols), f32),
            pltpu.VMEM((up, cols), f32),
            pltpu.VMEM((wide, cols), bf16),
            pltpu.VMEM((up, cols), f32),
            pltpu.VMEM((up, 128), f32),
            pltpu.VMEM((up, 128), f32),
            pltpu.VMEM((n_scen, 16, lanes), bf16),
            pltpu.VMEM((PASSES, 2, up // 4, 128), f32),
            pltpu.VMEM((PASSES, 2, up // 4, 128), f32),
            pltpu.VMEM((H_DEV, up), f32),
            pltpu.VMEM((n_scen, H_DEV, up), f32),
            pltpu.VMEM((1, cols), f32),
            dma((n_scen * 4,)),
            dma((5, n_scen * 4)),
            dma((n_scen,)),
            dma((n_scen,)),
            dma((PASSES, 2)),
            dma((PASSES, 2)),
            dma((n_scen,)),
            dma((n_scen,)),
        ],
        compiler_params=pltpu.CompilerParams(collective_id=0, has_side_effects=True, vmem_limit_bytes=56 * 1024 * 1024),
    )(sel, table, prior_dispatch, prior_commitment, cons, prior_multiplier, wind_output, need, ut)


def passed_along(value, axis, steps):
    count = lax.axis_size(axis)
    first, last = (max(0, -steps), min(count, count - steps))
    return lax.ppermute(value, axis, [(source, source + steps) for source in range(first, last)])


def plain(prior_dispatch, prior_commitment, prior_consensus, prior_multiplier, flow_factors,
          unit_buses, wind_buses, wind_output, demand, load_flows, line_limits, unit_table):
    units, columns = prior_dispatch.shape
    block = columns // H_DEV
    linear, quadratic, capacity, ramp_limit, noload = (unit_table[i][:, None] for i in range(5))
    factors = jnp.dot(flow_factors, selection(unit_buses, wind_buses, flow_factors.shape[1], units, jnp.bfloat16),
                      preferred_element_type=jnp.float32).astype(jnp.bfloat16)
    wind_total = jnp.sum(wind_output.astype(jnp.float32), axis=0)
    needed = jnp.repeat(demand, block)
    target = jnp.repeat(prior_consensus, block, axis=1)
    first_block = lax.axis_index("tm") == 0
    last_block = lax.axis_index("tm") == lax.axis_size("tm") - 1
    power, commit = prior_dispatch, prior_commitment
    factors = lax.all_gather(factors, "scen", axis=0, tiled=True)
    hourly = jnp.repeat(lax.all_gather(load_flows, "scen", axis=0, tiled=True).astype(jnp.float32), block, axis=1)
    limit = lax.all_gather(line_limits, "scen", axis=0, tiled=True).astype(jnp.float32)[:, None]
    for _ in range(PASSES):
        extended = jnp.concatenate([power.astype(jnp.bfloat16), wind_output], axis=0)
        flows = jnp.dot(factors, extended, preferred_element_type=jnp.float32) - hourly
        excess = (flows - jnp.clip(flows, -limit, limit)).astype(jnp.bfloat16)
        back = lax.dot_general(factors[:, :units], excess, (((0,), (0,)), ((), ())), preferred_element_type=jnp.float32)
        before = passed_along(power[:, columns - block:], "tm", 1)
        after = passed_along(power[:, :block], "tm", -1)
        before = jnp.where(first_block, power[:, :block], before)
        after = jnp.where(last_block, power[:, columns - block:], after)
        rate = power - jnp.concatenate([before, power[:, :columns - block]], axis=1)
        coming = jnp.concatenate([power[:, block:], after], axis=1) - power
        over = rate - jnp.clip(rate, -ramp_limit, ramp_limit)
        following = coming - jnp.clip(coming, -ramp_limit, ramp_limit)
        balance = jnp.sum(power, axis=0) + wind_total - needed
        short = jnp.maximum(power - capacity * commit, 0.0)
        grad_power = (linear + 2.0 * quadratic * power + flow_weight * back + ramp_weight * (over - following)
                      + balance_weight * balance + short_weight * short)
        grad_commit = noload - short_weight * capacity * short + prior_multiplier + penalty * (commit - target)
        power, commit = (jnp.clip(power - step_power * grad_power, 0.0, capacity),
                         jnp.clip(commit - step_commit * grad_commit, 0.0, 1.0))
    sums = jnp.sum((commit + prior_multiplier / penalty).reshape(units, H_DEV, block), axis=2)
    totals = lax.psum(sums, "scen")
    consensus = jnp.clip(totals / (block * lax.axis_size("scen")), 0.0, 1.0)
    updated = prior_multiplier + penalty * (commit - jnp.repeat(consensus, block, axis=1))
    return power, commit, consensus, updated


def solution(mesh):
    n_tm, n_scen = mesh.shape["tm"], mesh.shape["scen"]

    def per_device(*args):
        rows, cols = args[4].shape[0], args[0].shape[1]
        fits = (n_tm == 4 and n_scen % 2 == 0 and rows % 64 == 0 and cols == 256
                and args[7].shape[0] % 128 == 0)
        if fits:
            return fused(n_tm, n_scen, *args)
        return plain(*args)

    both_axes = P(None, ("tm", "scen"))
    in_specs = (both_axes, both_axes, P(None, "tm"), both_axes, P("scen", None), P(), P(), both_axes,
                P("tm"), P("scen", "tm"), P("scen"), P())
    out_specs = (both_axes, both_axes, P(None, "tm"), both_axes)
    return jax.shard_map(per_device, mesh=mesh, in_specs=in_specs, out_specs=out_specs, check_vma=False)
```

```python
import functools

import jax
import jax.numpy as jnp
from jax import lax
from jax.experimental import pallas as pl
from jax.experimental.pallas import tpu as pltpu
from jax.sharding import PartitionSpec as P

PASSES = 3
H_DEV = 8
MESH = pl.DeviceIdType.MESH

flow_weight = 0.5
ramp_weight = 1.0
balance_weight = 0.004
short_weight = 2.0
penalty = 1.0
step_power = 0.2
step_commit = 0.3


def kernel(n_tm, n_scen, units, sel_ref, tab_ref, pd_ref, pc_ref, cons_ref, mu_ref, wind_ref, table_ref, need_ref,
           power_out, commit_out, cons_out,
           fac, fact, load, bound, exc, pw, cm, mult, target, ext, backs, bef, aft,
           tabs, esend, erecv, psend, precv, total_row, small, ut_ref,
           recv_sem, send_sem, tsend, trecv, esem_s, esem_r, psem_s, psem_r):
    rows = sel_ref.shape[0]
    quarter = rows // 4
    up = pw.shape[0]
    cols = pw.shape[1]
    block = cols // H_DEV
    chunk = 2 * rows
    n_z = n_scen // 2
    f32, bf16 = jnp.float32, jnp.bfloat16
    tm = lax.axis_index("tm")
    scen = lax.axis_index("scen")
    y, c = tm // 2, tm % 2
    z, x = scen // 2, scen % 2
    oy = 1 - y
    oc = 1 - c
    ox = 1 - x
    mine = y * 2 + c
    other = oy * 2 + c
    dev_x = (tm, z * 2 + ox)
    dev_y = (oy * 2 + c, scen)
    dev_c = (y * 2 + oc, scen)
    dev_dn = (tm, scen - 2)
    dev_up = (tm, scen + 2)

    def piece(zz, xx, q):
        return (zz * 2 + xx) * 4 + q

    def at(p):
        return fac.at[pl.ds(pl.multiple_of(p * quarter, 16), quarter), :]

    def own(q):
        return sel_ref.at[pl.ds(pl.multiple_of(q * quarter, 16), quarter), :]

    def copy(src, p, slot, dev):
        return pltpu.make_async_remote_copy(
            src_ref=src, dst_ref=at(p), send_sem=send_sem.at[slot, p], recv_sem=recv_sem.at[p],
            device_id=dev, device_id_type=MESH)

    def pass_on(p, slot, dev):
        copy(at(p), p, slot, dev).start()

    def arrived(p):
        copy(at(p), p, 0, dev_x).wait_recv()

    def table_copy(k):
        peer = lax.rem(scen + k, n_scen)
        return pltpu.make_async_remote_copy(
            src_ref=tab_ref, dst_ref=tabs.at[scen], send_sem=tsend.at[k], recv_sem=trecv.at[scen],
            device_id=(tm, peer), device_id_type=MESH)

    barrier = pltpu.get_barrier_semaphore()
    for k in range(1, n_scen):
        pl.semaphore_signal(barrier, inc=1, device_id=(tm, lax.rem(scen + k, n_scen)), device_id_type=MESH)
    for k in range(1, n_tm):
        pl.semaphore_signal(barrier, inc=1, device_id=(lax.rem(tm + k, n_tm), scen), device_id_type=MESH)
    pl.semaphore_wait(barrier, n_scen - 1 + n_tm - 1)

    p_own = piece(z, x, mine)
    p_own2 = piece(z, x, other)

    @pl.when(z > 0)
    def _():
        copy(own(mine), p_own, 0, dev_dn).start()

    @pl.when(z < n_z - 1)
    def _():
        copy(own(mine), p_own, 1, dev_up).start()

    copy(own(mine), p_own, 2, dev_x).start()
    copy(own(other), p_own2, 2, dev_x).start()
    for k in range(1, n_scen):
        table_copy(k).start()

    def edges_of(tile_last, tile_first):
        lane = lax.broadcasted_iota(jnp.int32, (up // 4, 128), 1)
        last = jnp.zeros((up // 4, 128), f32)
        first = jnp.zeros((up // 4, 128), f32)
        for g in range(4):
            inside = (lane >= 32 * g) & (lane < 32 * g + 32)
            a = tile_last[g * (up // 4):(g + 1) * (up // 4), :]
            b = tile_first[g * (up // 4):(g + 1) * (up // 4), :]
            sa = (32 * g - 96) % 128
            sb = (32 * g) % 128
            a = pltpu.roll(a, sa, 1) if sa else a
            b = pltpu.roll(b, sb, 1) if sb else b
            last = jnp.where(inside, a, last)
            first = jnp.where(inside, b, first)
        return last, first

    def edge_copy(number, way):
        dev = (tm + 1, scen) if way == 0 else (tm - 1, scen)
        return pltpu.make_async_remote_copy(
            src_ref=esend.at[number, way], dst_ref=erecv.at[number, way],
            send_sem=esem_s.at[number, way], recv_sem=esem_r.at[number, way],
            device_id=dev, device_id_type=MESH)

    def send_edges(number):
        @pl.when(tm < n_tm - 1)
        def _():
            edge_copy(number, 0).start()

        @pl.when(tm > 0)
        def _():
            edge_copy(number, 1).start()

    def store_edges(number):
        last, first = edges_of(pw[:, cols - 128:], pw[:, :128])
        esend[number, 0] = last
        esend[number, 1] = first

    zero_tail = jnp.zeros((up - units, cols), f32)
    pw[:units, :] = pd_ref[...]
    pw[units:, :] = zero_tail
    store_edges(0)
    cm[:units, :] = pc_ref[...]
    cm[units:, :] = zero_tail
    mult[:units, :] = mu_ref[...]
    mult[units:, :] = zero_tail
    hour_row = lax.broadcasted_iota(jnp.int32, (H_DEV, cols), 0)
    hour_col = lax.broadcasted_iota(jnp.int32, (H_DEV, cols), 1)
    hour_of = ((hour_col >= hour_row * block) & (hour_col < hour_row * block + block)).astype(f32)
    small[...] = jnp.zeros_like(small)
    small[:, :units] = cons_ref[...]
    target[...] = jnp.dot(small[...].T, hour_of, preferred_element_type=f32, precision=lax.Precision.HIGHEST)
    small[...] = jnp.zeros_like(small)
    small[:table_ref.shape[0], :units] = table_ref[...]
    ut_ref[...] = small[...].T
    fac[pl.ds(pl.multiple_of(scen * rows, 16), rows), :] = sel_ref[...]
    tabs[scen] = tab_ref[...]
    ext[:up, :] = pw[...].astype(bf16)
    ext[up:, :] = wind_ref[...]
    needed = jnp.zeros((1, cols), f32)
    for h in range(H_DEV):
        needed = jnp.where(hour_of[h:h + 1] > 0.0, need_ref[h], needed)
    total_row[...] = jnp.sum(wind_ref[...].astype(f32), axis=0, keepdims=True) - needed
    send_edges(0)
    backs[...] = jnp.zeros((up, cols), f32)

    def along_z(k):
        for down in (True, False):
            zz = z - k if down else z + k
            ok = zz >= 0 if down else zz < n_z

            @pl.when(ok)
            def _():
                p = piece(zz, x, mine)
                arrived(p)
                if down:
                    @pl.when(z < n_z - 1)
                    def _():
                        pass_on(p, 1, dev_up)
                else:
                    @pl.when(z > 0)
                    def _():
                        pass_on(p, 0, dev_dn)
                pass_on(p, 2, dev_x)
                pass_on(p, 3, dev_y)
                pass_on(p, 4, dev_c)

    def both(k, f):
        @pl.when(z - k >= 0)
        def _():
            f(z - k)

        @pl.when(z + k < n_z)
        def _():
            f(z + k)

    def across_x(zz):
        p = piece(zz, ox, mine)
        arrived(p)
        pass_on(p, 3, dev_y)
        pass_on(p, 4, dev_c)

    def from_y_same(zz):
        p = piece(zz, x, other)
        arrived(p)
        pass_on(p, 4, dev_c)

    def from_y_cross(zz):
        p = piece(zz, ox, other)
        arrived(p)
        pass_on(p, 4, dev_c)

    def own_plane_x():
        for q in (mine, other):
            p = piece(z, ox, q)
            arrived(p)
            pass_on(p, 4, dev_c)

    def table_arrived(src):
        pltpu.make_async_remote_copy(
            src_ref=tab_ref, dst_ref=tabs.at[src], send_sem=tsend.at[0], recv_sem=trecv.at[src],
            device_id=dev_x, device_id_type=MESH).wait_recv()

    spread_row = lax.broadcasted_iota(jnp.int32, (H_DEV, cols), 0)
    spread_col = lax.broadcasted_iota(jnp.int32, (H_DEV, cols), 1)
    load_of = ((spread_col >= spread_row * block) & (spread_col < spread_row * block + block)).astype(bf16)
    lines_first = (((0,), (0,)), ((), ()))

    def line_step(at_rows):
        flows = jnp.dot(fac[at_rows, :], ext[...], preferred_element_type=f32) - load[at_rows, :]
        lim = bound[at_rows, :]
        exc[at_rows, :] = (flows - jnp.clip(flows, -lim, lim)).astype(bf16)

    def process(zz):
        for xx in range(2):
            s = zz * 2 + xx
            at_rows = pl.ds(pl.multiple_of(s * rows, 16), rows)
            load[at_rows, :] = lax.dot_general(tabs[s], load_of, lines_first, preferred_element_type=f32)
            bound[at_rows, :] = jnp.broadcast_to(fac[at_rows, units:units + 1].astype(f32), (rows, cols))
        at_rows = pl.ds(pl.multiple_of(zz * chunk, 128), chunk)
        fact[:, at_rows] = fac[at_rows, :up].T
        line_step(at_rows)
        backs[...] += jnp.dot(fact[:, at_rows], exc[at_rows, :], preferred_element_type=f32)

    def from_core(zz):
        for xx in range(2):
            for yy in range(2):
                arrived(piece(zz, xx, yy * 2 + oc))
            table_arrived(zz * 2 + xx)
        process(zz)

    def own_chunk():
        for q in (oc, 2 + oc):
            arrived(piece(z, ox, q))
        table_arrived(z * 2 + ox)
        process(z)

    along_z(1)
    own_plane_x()
    for k in range(2, n_z + 1):
        if k < n_z:
            along_z(k)
        both(k - 1, across_x)
        both(k - 1, from_y_same)
        if k > 2:
            both(k - 2, from_y_cross)
            both(k - 2, from_core)
        else:
            own_chunk()
    both(n_z - 1, from_y_cross)
    both(n_z - 1, from_core)

    tile = 32
    lane = lax.broadcasted_iota(jnp.int32, (tile, cols), 1)
    for number in range(PASSES):
        if number > 0:
            send_edges(number)
            for k in range(n_z):
                line_step(pl.ds(k * chunk, chunk))
            backs[...] = jnp.dot(fact[...], exc[...], preferred_element_type=f32)

        @pl.when(tm > 0)
        def _():
            edge_copy(number, 0).wait_recv()
            for g in range(4):
                e = erecv[number, 0]
                s = (-32 * g) % 128
                bef[g * (up // 4):(g + 1) * (up // 4), :] = pltpu.roll(e, s, 1) if s else e

        @pl.when(tm == 0)
        def _():
            bef[...] = pw[:, :128]

        @pl.when(tm < n_tm - 1)
        def _():
            edge_copy(number, 1).wait_recv()
            for g in range(4):
                e = erecv[number, 1]
                s = (96 - 32 * g) % 128
                aft[g * (up // 4):(g + 1) * (up // 4), :] = pltpu.roll(e, s, 1) if s else e

        @pl.when(tm == n_tm - 1)
        def _():
            aft[...] = pw[:, cols - 128:]

        balance = jnp.sum(pw[...], axis=0, keepdims=True) + total_row[...]
        balance_part = balance_weight * balance

        def update(i, carry):
            r = pl.ds(pl.multiple_of(i * tile, tile), tile)
            power = pw[r, :]
            commit = cm[r, :]
            linear = ut_ref[r, 0:1]
            quadratic = ut_ref[r, 1:2]
            capacity = ut_ref[r, 2:3]
            ramp_limit = ut_ref[r, 3:4]
            noload = ut_ref[r, 4:5]
            b = bef[r, :]
            a = aft[r, :]
            previous = jnp.where(lane < block, jnp.concatenate([b] * (cols // 128), axis=1), pltpu.roll(power, block, 1))
            nxt = jnp.where(lane >= cols - block, jnp.concatenate([a] * (cols // 128), axis=1), pltpu.roll(power, cols - block, 1))
            rate = power - previous
            over = rate - jnp.clip(rate, -ramp_limit, ramp_limit)
            coming = nxt - power
            following = coming - jnp.clip(coming, -ramp_limit, ramp_limit)
            ramp_term = over - following
            short = jnp.maximum(power - capacity * commit, 0.0)
            grad_power = (linear + 2.0 * quadratic * power + flow_weight * backs[r, :] + ramp_weight * ramp_term
                          + balance_part + short_weight * short)
            grad_commit = noload - short_weight * capacity * short + mult[r, :] + penalty * (commit - target[r, :])
            new_power = jnp.clip(power - step_power * grad_power, 0.0, capacity)
            pw[r, :] = new_power
            cm[r, :] = jnp.clip(commit - step_commit * grad_commit, 0.0, 1.0)
            ext[r, :] = new_power.astype(bf16)
            return carry

        lax.fori_loop(0, up // tile, update, 0)
        if number < PASSES - 1:
            store_edges(number + 1)

    psend[...] = lax.dot_general(hour_of, cm[...] + mult[...] / penalty, (((1,), (1,)), ((), ())),
                                 preferred_element_type=f32, precision=lax.Precision.HIGHEST)
    power_out[...] = pw[:units, :]
    commit_out[...] = cm[:units, :]

    def sum_copy(k):
        return pltpu.make_async_remote_copy(
            src_ref=psend, dst_ref=precv.at[scen], send_sem=psem_s.at[k], recv_sem=psem_r.at[scen],
            device_id=(tm, lax.rem(scen + k, n_scen)), device_id_type=MESH)

    for k in range(1, n_scen):
        sum_copy(k).start()
    precv[scen] = psend[...]
    for k in range(1, n_scen):
        src = lax.rem(scen + k, n_scen)
        pltpu.make_async_remote_copy(
            src_ref=psend, dst_ref=precv.at[src], send_sem=psem_s.at[k], recv_sem=psem_r.at[src],
            device_id=dev_x, device_id_type=MESH).wait_recv()
    totals = precv[0]
    for k in range(1, n_scen):
        totals = totals + precv[k]
    consensus = jnp.clip(totals / (block * n_scen), 0.0, 1.0)
    cons_out[...] = consensus

    @pl.when(z > 0)
    def _():
        copy(own(mine), p_own, 0, dev_dn).wait_send()

    @pl.when(z < n_z - 1)
    def _():
        copy(own(mine), p_own, 1, dev_up).wait_send()

    copy(own(mine), p_own, 2, dev_x).wait_send()
    copy(own(other), p_own2, 2, dev_x).wait_send()

    def left(p, slot, dev):
        copy(at(p), p, slot, dev).wait_send()

    for k in range(1, n_z):
        for down in (True, False):
            zz = z - k if down else z + k

            @pl.when(zz >= 0 if down else zz < n_z)
            def _():
                p = piece(zz, x, mine)
                if down:
                    @pl.when(z < n_z - 1)
                    def _():
                        left(p, 1, dev_up)
                else:
                    @pl.when(z > 0)
                    def _():
                        left(p, 0, dev_dn)
                left(p, 2, dev_x)
                left(p, 3, dev_y)
                left(p, 4, dev_c)
                p = piece(zz, ox, mine)
                left(p, 3, dev_y)
                left(p, 4, dev_c)
                left(piece(zz, x, other), 4, dev_c)
                left(piece(zz, ox, other), 4, dev_c)
    for q in (mine, other):
        left(piece(z, ox, q), 4, dev_c)
    for k in range(1, n_scen):
        table_copy(k).wait_send()
        sum_copy(k).wait_send()
    for number in range(PASSES):
        @pl.when(tm < n_tm - 1)
        def _():
            edge_copy(number, 0).wait_send()

        @pl.when(tm > 0)
        def _():
            edge_copy(number, 1).wait_send()


def selection(unit_buses, wind_buses, buses, up, dtype):
    units = unit_buses.shape[0]
    wanted = jnp.concatenate([unit_buses, jnp.full((up - units,), -1, unit_buses.dtype), wind_buses])
    return (lax.broadcasted_iota(jnp.int32, (buses, wanted.shape[0]), 0) == wanted[None, :]).astype(dtype)


def finish(units, power_ref, commit_ref, mult_ref, cons_ref, power_out, commit_out, cons_out, upd_out):
    cols = mult_ref.shape[1]
    block = cols // H_DEV
    hour_row = lax.broadcasted_iota(jnp.int32, (H_DEV, cols), 0)
    hour_col = lax.broadcasted_iota(jnp.int32, (H_DEV, cols), 1)
    hour_of = ((hour_col >= hour_row * block) & (hour_col < hour_row * block + block)).astype(jnp.float32)
    wide = jnp.dot(cons_ref[...].T, hour_of, preferred_element_type=jnp.float32, precision=lax.Precision.HIGHEST)
    power_out[...] = power_ref[...]
    commit = commit_ref[...]
    commit_out[...] = commit
    cons_out[...] = cons_ref[:, :units]
    upd_out[...] = mult_ref[...] + penalty * (commit - wide[:units, :])


def fused(n_tm, n_scen, prior_dispatch, prior_commitment, prior_consensus, prior_multiplier, flow_factors,
          unit_buses, wind_buses, wind_output, demand, load_flows, line_limits, unit_table):
    units, cols = prior_dispatch.shape
    rows, buses = flow_factors.shape
    farms = wind_output.shape[0]
    up = -(-units // 128) * 128
    f32, bf16 = jnp.float32, jnp.bfloat16
    sel = jnp.dot(flow_factors, selection(unit_buses, wind_buses, buses, up, bf16), preferred_element_type=f32).astype(bf16)
    column = lax.broadcasted_iota(jnp.int32, sel.shape, 1)
    sel = jnp.where(column == units, line_limits[:, None], sel)
    lines = rows * n_scen
    wide = up + farms
    vm = pl.BlockSpec(memory_space=pltpu.VMEM)
    dma = pltpu.SemaphoreType.DMA
    power, commit, cons = pl.pallas_call(
        functools.partial(kernel, n_tm, n_scen, units),
        name="window",
        out_shape=(
            jax.ShapeDtypeStruct((units, cols), f32),
            jax.ShapeDtypeStruct((units, cols), f32),
            jax.ShapeDtypeStruct((H_DEV, up), f32),
        ),
        in_specs=[vm] * 8 + [pl.BlockSpec(memory_space=pltpu.SMEM)],
        out_specs=(vm,) * 3,
        scratch_shapes=[
            pltpu.VMEM((lines, wide), bf16),
            pltpu.VMEM((up, lines), bf16),
            pltpu.VMEM((lines, cols), f32),
            pltpu.VMEM((lines, cols), f32),
            pltpu.VMEM((lines, cols), bf16),
            pltpu.VMEM((up, cols), f32),
            pltpu.VMEM((up, cols), f32),
            pltpu.VMEM((up, cols), f32),
            pltpu.VMEM((up, cols), f32),
            pltpu.VMEM((wide, cols), bf16),
            pltpu.VMEM((up, cols), f32),
            pltpu.VMEM((up, 128), f32),
            pltpu.VMEM((up, 128), f32),
            pltpu.VMEM((n_scen, H_DEV, rows), bf16),
            pltpu.VMEM((PASSES, 2, up // 4, 128), f32),
            pltpu.VMEM((PASSES, 2, up // 4, 128), f32),
            pltpu.VMEM((H_DEV, up), f32),
            pltpu.VMEM((n_scen, H_DEV, up), f32),
            pltpu.VMEM((1, cols), f32),
            pltpu.VMEM((H_DEV, up), f32),
            pltpu.VMEM((up, H_DEV), f32),
            dma((n_scen * 4,)),
            dma((5, n_scen * 4)),
            dma((n_scen,)),
            dma((n_scen,)),
            dma((PASSES, 2)),
            dma((PASSES, 2)),
            dma((n_scen,)),
            dma((n_scen,)),
        ],
        compiler_params=pltpu.CompilerParams(collective_id=0, has_side_effects=True, vmem_limit_bytes=56 * 1024 * 1024),
    )(sel, load_flows.T, prior_dispatch, prior_commitment, prior_consensus.T, prior_multiplier, wind_output, unit_table, demand)
    power, commit, cons, updated = pl.pallas_call(
        functools.partial(finish, units),
        name="finish",
        out_shape=(
            jax.ShapeDtypeStruct((units, cols), f32),
            jax.ShapeDtypeStruct((units, cols), f32),
            jax.ShapeDtypeStruct((H_DEV, units), f32),
            jax.ShapeDtypeStruct((units, cols), f32),
        ),
        in_specs=[vm] * 4,
        out_specs=(vm,) * 4,
    )(power, commit, prior_multiplier, cons)
    return power, commit, cons.T, updated


def passed_along(value, axis, steps):
    count = lax.axis_size(axis)
    first, last = (max(0, -steps), min(count, count - steps))
    return lax.ppermute(value, axis, [(source, source + steps) for source in range(first, last)])


def plain(prior_dispatch, prior_commitment, prior_consensus, prior_multiplier, flow_factors,
          unit_buses, wind_buses, wind_output, demand, load_flows, line_limits, unit_table):
    units, columns = prior_dispatch.shape
    block = columns // H_DEV
    linear, quadratic, capacity, ramp_limit, noload = (unit_table[i][:, None] for i in range(5))
    factors = jnp.dot(flow_factors, selection(unit_buses, wind_buses, flow_factors.shape[1], units, jnp.bfloat16),
                      preferred_element_type=jnp.float32).astype(jnp.bfloat16)
    wind_total = jnp.sum(wind_output.astype(jnp.float32), axis=0)
    needed = jnp.repeat(demand, block)
    target = jnp.repeat(prior_consensus, block, axis=1)
    first_block = lax.axis_index("tm") == 0
    last_block = lax.axis_index("tm") == lax.axis_size("tm") - 1
    power, commit = prior_dispatch, prior_commitment
    factors = lax.all_gather(factors, "scen", axis=0, tiled=True)
    hourly = jnp.repeat(lax.all_gather(load_flows, "scen", axis=0, tiled=True).astype(jnp.float32), block, axis=1)
    limit = lax.all_gather(line_limits, "scen", axis=0, tiled=True).astype(jnp.float32)[:, None]
    for _ in range(PASSES):
        extended = jnp.concatenate([power.astype(jnp.bfloat16), wind_output], axis=0)
        flows = jnp.dot(factors, extended, preferred_element_type=jnp.float32) - hourly
        excess = (flows - jnp.clip(flows, -limit, limit)).astype(jnp.bfloat16)
        back = lax.dot_general(factors[:, :units], excess, (((0,), (0,)), ((), ())), preferred_element_type=jnp.float32)
        before = passed_along(power[:, columns - block:], "tm", 1)
        after = passed_along(power[:, :block], "tm", -1)
        before = jnp.where(first_block, power[:, :block], before)
        after = jnp.where(last_block, power[:, columns - block:], after)
        rate = power - jnp.concatenate([before, power[:, :columns - block]], axis=1)
        coming = jnp.concatenate([power[:, block:], after], axis=1) - power
        over = rate - jnp.clip(rate, -ramp_limit, ramp_limit)
        following = coming - jnp.clip(coming, -ramp_limit, ramp_limit)
        balance = jnp.sum(power, axis=0) + wind_total - needed
        short = jnp.maximum(power - capacity * commit, 0.0)
        grad_power = (linear + 2.0 * quadratic * power + flow_weight * back + ramp_weight * (over - following)
                      + balance_weight * balance + short_weight * short)
        grad_commit = noload - short_weight * capacity * short + prior_multiplier + penalty * (commit - target)
        power, commit = (jnp.clip(power - step_power * grad_power, 0.0, capacity),
                         jnp.clip(commit - step_commit * grad_commit, 0.0, 1.0))
    sums = jnp.sum((commit + prior_multiplier / penalty).reshape(units, H_DEV, block), axis=2)
    totals = lax.psum(sums, "scen")
    consensus = jnp.clip(totals / (block * lax.axis_size("scen")), 0.0, 1.0)
    updated = prior_multiplier + penalty * (commit - jnp.repeat(consensus, block, axis=1))
    return power, commit, consensus, updated


def solution(mesh):
    n_tm, n_scen = mesh.shape["tm"], mesh.shape["scen"]

    def per_device(*args):
        rows, cols = args[4].shape[0], args[0].shape[1]
        fits = (n_tm == 4 and n_scen % 2 == 0 and rows % 64 == 0 and cols == 256
                and args[7].shape[0] % 128 == 0 and args[0].shape[0] % 128 > 0)
        if fits:
            return fused(n_tm, n_scen, *args)
        return plain(*args)

    both_axes = P(None, ("tm", "scen"))
    in_specs = (both_axes, both_axes, P(None, "tm"), both_axes, P("scen", None), P(), P(), both_axes,
                P("tm"), P("scen", "tm"), P("scen"), P())
    out_specs = (both_axes, both_axes, P(None, "tm"), both_axes)
    return jax.shard_map(per_device, mesh=mesh, in_specs=in_specs, out_specs=out_specs, check_vma=False)
```

```python
import functools

import jax
import jax.numpy as jnp
from jax import lax
from jax.experimental import pallas as pl
from jax.experimental.pallas import tpu as pltpu
from jax.sharding import PartitionSpec as P

PASSES = 3
H_DEV = 8
MESH = pl.DeviceIdType.MESH

flow_weight = 0.5
ramp_weight = 1.0
balance_weight = 0.004
short_weight = 2.0
penalty = 1.0
step_power = 0.2
step_commit = 0.3


def split(value):
    high = value.astype(jnp.bfloat16)
    rest = value - high.astype(jnp.float32)
    middle = rest.astype(jnp.bfloat16)
    return high, middle, (rest - middle.astype(jnp.float32)).astype(jnp.bfloat16)


def kernel(n_tm, n_scen, units, sel_ref, tab_ref, pd_ref, pc_ref, cons_ref, mu_ref, wind_ref, table_ref, need_ref,
           power_out, commit_out, cons_out,
           fac, fact, load, bound, exc, pw, cm, mult, target, ext, backs, bef, aft,
           tabs, esend, erecv, psend, precv, total_row, small, ut_ref,
           recv_sem, send_sem, tsend, trecv, esem_s, esem_r, psem_s, psem_r):
    rows = sel_ref.shape[0]
    quarter = rows // 4
    up = pw.shape[0]
    cols = pw.shape[1]
    block = cols // H_DEV
    chunk = 2 * rows
    n_z = n_scen // 2
    f32, bf16 = jnp.float32, jnp.bfloat16
    tm = lax.axis_index("tm")
    scen = lax.axis_index("scen")
    y, c = tm // 2, tm % 2
    z, x = scen // 2, scen % 2
    oy = 1 - y
    oc = 1 - c
    ox = 1 - x
    mine = y * 2 + c
    other = oy * 2 + c
    dev_x = (tm, z * 2 + ox)
    dev_y = (oy * 2 + c, scen)
    dev_c = (y * 2 + oc, scen)
    dev_dn = (tm, scen - 2)
    dev_up = (tm, scen + 2)

    def piece(zz, xx, q):
        return (zz * 2 + xx) * 4 + q

    def at(p):
        return fac.at[pl.ds(pl.multiple_of(p * quarter, 16), quarter), :]

    def own(q):
        return sel_ref.at[pl.ds(pl.multiple_of(q * quarter, 16), quarter), :]

    def copy(src, p, slot, dev):
        return pltpu.make_async_remote_copy(
            src_ref=src, dst_ref=at(p), send_sem=send_sem.at[slot, p], recv_sem=recv_sem.at[p],
            device_id=dev, device_id_type=MESH)

    def pass_on(p, slot, dev):
        copy(at(p), p, slot, dev).start()

    def arrived(p):
        copy(at(p), p, 0, dev_x).wait_recv()

    def table_copy(k):
        peer = lax.rem(scen + k, n_scen)
        return pltpu.make_async_remote_copy(
            src_ref=tab_ref, dst_ref=tabs.at[scen], send_sem=tsend.at[k], recv_sem=trecv.at[scen],
            device_id=(tm, peer), device_id_type=MESH)

    barrier = pltpu.get_barrier_semaphore()
    for k in range(1, n_scen):
        pl.semaphore_signal(barrier, inc=1, device_id=(tm, lax.rem(scen + k, n_scen)), device_id_type=MESH)
    for k in range(1, n_tm):
        pl.semaphore_signal(barrier, inc=1, device_id=(lax.rem(tm + k, n_tm), scen), device_id_type=MESH)
    pl.semaphore_wait(barrier, n_scen - 1 + n_tm - 1)

    p_own = piece(z, x, mine)
    p_own2 = piece(z, x, other)

    @pl.when(z > 0)
    def _():
        copy(own(mine), p_own, 0, dev_dn).start()

    @pl.when(z < n_z - 1)
    def _():
        copy(own(mine), p_own, 1, dev_up).start()

    copy(own(mine), p_own, 2, dev_x).start()
    copy(own(other), p_own2, 2, dev_x).start()
    for k in range(1, n_scen):
        table_copy(k).start()

    def edges_of(tile_last, tile_first):
        lane = lax.broadcasted_iota(jnp.int32, (up // 4, 128), 1)
        last = jnp.zeros((up // 4, 128), f32)
        first = jnp.zeros((up // 4, 128), f32)
        for g in range(4):
            inside = (lane >= 32 * g) & (lane < 32 * g + 32)
            a = tile_last[g * (up // 4):(g + 1) * (up // 4), :]
            b = tile_first[g * (up // 4):(g + 1) * (up // 4), :]
            sa = (32 * g - 96) % 128
            sb = (32 * g) % 128
            a = pltpu.roll(a, sa, 1) if sa else a
            b = pltpu.roll(b, sb, 1) if sb else b
            last = jnp.where(inside, a, last)
            first = jnp.where(inside, b, first)
        return last, first

    def edge_copy(number, way):
        dev = (tm + 1, scen) if way == 0 else (tm - 1, scen)
        return pltpu.make_async_remote_copy(
            src_ref=esend.at[number, way], dst_ref=erecv.at[number, way],
            send_sem=esem_s.at[number, way], recv_sem=esem_r.at[number, way],
            device_id=dev, device_id_type=MESH)

    def send_edges(number):
        @pl.when(tm < n_tm - 1)
        def _():
            edge_copy(number, 0).start()

        @pl.when(tm > 0)
        def _():
            edge_copy(number, 1).start()

    def store_edges(number):
        last, first = edges_of(pw[:, cols - 128:], pw[:, :128])
        esend[number, 0] = last
        esend[number, 1] = first

    zero_tail = jnp.zeros((up - units, cols), f32)
    pw[:units, :] = pd_ref[...]
    pw[units:, :] = zero_tail
    store_edges(0)
    cm[:units, :] = pc_ref[...]
    cm[units:, :] = zero_tail
    mult[:units, :] = mu_ref[...]
    mult[units:, :] = zero_tail
    hour_row = lax.broadcasted_iota(jnp.int32, (H_DEV, cols), 0)
    hour_col = lax.broadcasted_iota(jnp.int32, (H_DEV, cols), 1)
    hour_of = ((hour_col >= hour_row * block) & (hour_col < hour_row * block + block)).astype(f32)
    small[...] = jnp.zeros_like(small)
    small[:, :units] = cons_ref[...]
    target[...] = jnp.dot(small[...].T, hour_of, preferred_element_type=f32, precision=lax.Precision.HIGHEST)
    small[...] = jnp.zeros_like(small)
    small[:table_ref.shape[0], :units] = table_ref[...]
    ut_ref[...] = small[...].T
    fac[pl.ds(pl.multiple_of(scen * rows, 16), rows), :] = sel_ref[...]
    tabs[scen] = tab_ref[...]
    ext[:up, :] = pw[...].astype(bf16)
    ext[up:, :] = wind_ref[...]
    needed = jnp.zeros((1, cols), f32)
    for h in range(H_DEV):
        needed = jnp.where(hour_of[h:h + 1] > 0.0, need_ref[h], needed)
    total_row[...] = jnp.sum(wind_ref[...].astype(f32), axis=0, keepdims=True) - needed
    send_edges(0)
    backs[...] = jnp.zeros((up, cols), f32)

    def along_z(k):
        for down in (True, False):
            zz = z - k if down else z + k
            ok = zz >= 0 if down else zz < n_z

            @pl.when(ok)
            def _():
                p = piece(zz, x, mine)
                arrived(p)
                if down:
                    @pl.when(z < n_z - 1)
                    def _():
                        pass_on(p, 1, dev_up)
                else:
                    @pl.when(z > 0)
                    def _():
                        pass_on(p, 0, dev_dn)
                pass_on(p, 2, dev_x)
                pass_on(p, 3, dev_y)
                pass_on(p, 4, dev_c)

    def both(k, f):
        @pl.when(z - k >= 0)
        def _():
            f(z - k)

        @pl.when(z + k < n_z)
        def _():
            f(z + k)

    def across_x(zz):
        p = piece(zz, ox, mine)
        arrived(p)
        pass_on(p, 3, dev_y)
        pass_on(p, 4, dev_c)

    def from_y_same(zz):
        p = piece(zz, x, other)
        arrived(p)
        pass_on(p, 4, dev_c)

    def from_y_cross(zz):
        p = piece(zz, ox, other)
        arrived(p)
        pass_on(p, 4, dev_c)

    def own_plane_x():
        for q in (mine, other):
            p = piece(z, ox, q)
            arrived(p)
            pass_on(p, 4, dev_c)

    def table_arrived(src):
        pltpu.make_async_remote_copy(
            src_ref=tab_ref, dst_ref=tabs.at[src], send_sem=tsend.at[0], recv_sem=trecv.at[src],
            device_id=dev_x, device_id_type=MESH).wait_recv()

    spread_row = lax.broadcasted_iota(jnp.int32, (H_DEV, cols), 0)
    spread_col = lax.broadcasted_iota(jnp.int32, (H_DEV, cols), 1)
    load_of = ((spread_col >= spread_row * block) & (spread_col < spread_row * block + block)).astype(bf16)
    lines_first = (((0,), (0,)), ((), ()))

    def line_step(at_rows):
        flows = jnp.dot(fac[at_rows, :], ext[...], preferred_element_type=f32) - load[at_rows, :]
        lim = bound[at_rows, :]
        exc[at_rows, :] = (flows - jnp.clip(flows, -lim, lim)).astype(bf16)

    def process(zz):
        for xx in range(2):
            s = zz * 2 + xx
            at_rows = pl.ds(pl.multiple_of(s * rows, 16), rows)
            load[at_rows, :] = lax.dot_general(tabs[s], load_of, lines_first, preferred_element_type=f32)
            bound[at_rows, :] = jnp.broadcast_to(fac[at_rows, units:units + 1].astype(f32), (rows, cols))
        at_rows = pl.ds(pl.multiple_of(zz * chunk, 128), chunk)
        fact[:, at_rows] = fac[at_rows, :up].T
        line_step(at_rows)
        backs[...] += jnp.dot(fact[:, at_rows], exc[at_rows, :], preferred_element_type=f32)

    def from_core(zz):
        for xx in range(2):
            for yy in range(2):
                arrived(piece(zz, xx, yy * 2 + oc))
            table_arrived(zz * 2 + xx)
        process(zz)

    def own_chunk():
        for q in (oc, 2 + oc):
            arrived(piece(z, ox, q))
        table_arrived(z * 2 + ox)
        process(z)

    along_z(1)
    own_plane_x()
    for k in range(2, n_z + 1):
        if k < n_z:
            along_z(k)
        both(k - 1, across_x)
        both(k - 1, from_y_same)
        if k > 2:
            both(k - 2, from_y_cross)
            both(k - 2, from_core)
        else:
            own_chunk()
    both(n_z - 1, from_y_cross)
    both(n_z - 1, from_core)

    tile = 32
    lane = lax.broadcasted_iota(jnp.int32, (tile, cols), 1)
    for number in range(PASSES):
        if number > 0:
            send_edges(number)
            for k in range(n_z):
                line_step(pl.ds(k * chunk, chunk))
            backs[...] = jnp.dot(fact[...], exc[...], preferred_element_type=f32)

        @pl.when(tm > 0)
        def _():
            edge_copy(number, 0).wait_recv()
            for g in range(4):
                e = erecv[number, 0]
                s = (-32 * g) % 128
                bef[g * (up // 4):(g + 1) * (up // 4), :] = pltpu.roll(e, s, 1) if s else e

        @pl.when(tm == 0)
        def _():
            bef[...] = pw[:, :128]

        @pl.when(tm < n_tm - 1)
        def _():
            edge_copy(number, 1).wait_recv()
            for g in range(4):
                e = erecv[number, 1]
                s = (96 - 32 * g) % 128
                aft[g * (up // 4):(g + 1) * (up // 4), :] = pltpu.roll(e, s, 1) if s else e

        @pl.when(tm == n_tm - 1)
        def _():
            aft[...] = pw[:, cols - 128:]

        balance = jnp.sum(pw[...], axis=0, keepdims=True) + total_row[...]
        balance_part = balance_weight * balance

        def update(i, carry):
            r = pl.ds(pl.multiple_of(i * tile, tile), tile)
            power = pw[r, :]
            commit = cm[r, :]
            linear = ut_ref[r, 0:1]
            quadratic = ut_ref[r, 1:2]
            capacity = ut_ref[r, 2:3]
            ramp_limit = ut_ref[r, 3:4]
            noload = ut_ref[r, 4:5]
            b = bef[r, :]
            a = aft[r, :]
            previous = jnp.where(lane < block, jnp.concatenate([b] * (cols // 128), axis=1), pltpu.roll(power, block, 1))
            nxt = jnp.where(lane >= cols - block, jnp.concatenate([a] * (cols // 128), axis=1), pltpu.roll(power, cols - block, 1))
            rate = power - previous
            over = rate - jnp.clip(rate, -ramp_limit, ramp_limit)
            coming = nxt - power
            following = coming - jnp.clip(coming, -ramp_limit, ramp_limit)
            ramp_term = over - following
            short = jnp.maximum(power - capacity * commit, 0.0)
            grad_power = (linear + 2.0 * quadratic * power + flow_weight * backs[r, :] + ramp_weight * ramp_term
                          + balance_part + short_weight * short)
            grad_commit = noload - short_weight * capacity * short + mult[r, :] + penalty * (commit - target[r, :])
            new_power = jnp.clip(power - step_power * grad_power, 0.0, capacity)
            pw[r, :] = new_power
            cm[r, :] = jnp.clip(commit - step_commit * grad_commit, 0.0, 1.0)
            ext[r, :] = new_power.astype(bf16)
            return carry

        lax.fori_loop(0, up // tile, update, 0, unroll=4)
        if number < PASSES - 1:
            store_edges(number + 1)

    spread = hour_of.astype(bf16)
    sums = jnp.zeros((H_DEV, up), f32)
    for part in split(cm[...] + mult[...] / penalty):
        sums = sums + lax.dot_general(spread, part, (((1,), (1,)), ((), ())), preferred_element_type=f32)
    psend[...] = sums

    def sum_copy(k):
        return pltpu.make_async_remote_copy(
            src_ref=psend, dst_ref=precv.at[scen], send_sem=psem_s.at[k], recv_sem=psem_r.at[scen],
            device_id=(tm, lax.rem(scen + k, n_scen)), device_id_type=MESH)

    for k in range(1, n_scen):
        sum_copy(k).start()
    precv[scen] = psend[...]
    power_out[...] = pw[:units, :]
    commit_out[...] = cm[:units, :]
    for k in range(1, n_scen):
        src = lax.rem(scen + k, n_scen)
        pltpu.make_async_remote_copy(
            src_ref=psend, dst_ref=precv.at[src], send_sem=psem_s.at[k], recv_sem=psem_r.at[src],
            device_id=dev_x, device_id_type=MESH).wait_recv()
    totals = precv[0]
    for k in range(1, n_scen):
        totals = totals + precv[k]
    consensus = jnp.clip(totals / (block * n_scen), 0.0, 1.0)
    cons_out[...] = consensus

    @pl.when(z > 0)
    def _():
        copy(own(mine), p_own, 0, dev_dn).wait_send()

    @pl.when(z < n_z - 1)
    def _():
        copy(own(mine), p_own, 1, dev_up).wait_send()

    copy(own(mine), p_own, 2, dev_x).wait_send()
    copy(own(other), p_own2, 2, dev_x).wait_send()

    def left(p, slot, dev):
        copy(at(p), p, slot, dev).wait_send()

    for k in range(1, n_z):
        for down in (True, False):
            zz = z - k if down else z + k

            @pl.when(zz >= 0 if down else zz < n_z)
            def _():
                p = piece(zz, x, mine)
                if down:
                    @pl.when(z < n_z - 1)
                    def _():
                        left(p, 1, dev_up)
                else:
                    @pl.when(z > 0)
                    def _():
                        left(p, 0, dev_dn)
                left(p, 2, dev_x)
                left(p, 3, dev_y)
                left(p, 4, dev_c)
                p = piece(zz, ox, mine)
                left(p, 3, dev_y)
                left(p, 4, dev_c)
                left(piece(zz, x, other), 4, dev_c)
                left(piece(zz, ox, other), 4, dev_c)
    for q in (mine, other):
        left(piece(z, ox, q), 4, dev_c)
    for k in range(1, n_scen):
        table_copy(k).wait_send()
        sum_copy(k).wait_send()
    for number in range(PASSES):
        @pl.when(tm < n_tm - 1)
        def _():
            edge_copy(number, 0).wait_send()

        @pl.when(tm > 0)
        def _():
            edge_copy(number, 1).wait_send()


def selection(unit_buses, wind_buses, buses, up, dtype):
    units = unit_buses.shape[0]
    wanted = jnp.concatenate([unit_buses, jnp.full((up - units,), -1, unit_buses.dtype), wind_buses])
    return (lax.broadcasted_iota(jnp.int32, (buses, wanted.shape[0]), 0) == wanted[None, :]).astype(dtype)


def finish(units, power_ref, commit_ref, mult_ref, cons_ref, power_out, commit_out, cons_out, upd_out, parts):
    tile, cols = mult_ref.shape
    block = cols // H_DEV
    step = pl.program_id(0)

    @pl.when(step == 0)
    def _():
        cons = cons_ref[...]
        cons_out[...] = cons[:, :units]
        parts[...] = jnp.concatenate([part.astype(jnp.float32) for part in split(cons)], axis=0).T

    hour_row = lax.broadcasted_iota(jnp.int32, (H_DEV, cols), 0)
    hour_col = lax.broadcasted_iota(jnp.int32, (H_DEV, cols), 1)
    hour_of = ((hour_col >= hour_row * block) & (hour_col < hour_row * block + block)).astype(jnp.float32)
    spread = jnp.concatenate([hour_of] * 3, axis=0).astype(jnp.bfloat16)
    mine = parts[pl.ds(pl.multiple_of(step * tile, 8), tile), :].astype(jnp.bfloat16)
    wide = jnp.dot(mine, spread, preferred_element_type=jnp.float32)
    power_out[...] = power_ref[...]
    commit = commit_ref[...]
    commit_out[...] = commit
    upd_out[...] = mult_ref[...] + penalty * (commit - wide)


def fused(n_tm, n_scen, prior_dispatch, prior_commitment, prior_consensus, prior_multiplier, flow_factors,
          unit_buses, wind_buses, wind_output, demand, load_flows, line_limits, unit_table):
    units, cols = prior_dispatch.shape
    rows, buses = flow_factors.shape
    farms = wind_output.shape[0]
    up = -(-units // 128) * 128
    f32, bf16 = jnp.float32, jnp.bfloat16
    sel = jnp.dot(flow_factors, selection(unit_buses, wind_buses, buses, up, bf16), preferred_element_type=f32).astype(bf16)
    column = lax.broadcasted_iota(jnp.int32, sel.shape, 1)
    sel = jnp.where(column == units, line_limits[:, None], sel)
    lines = rows * n_scen
    wide = up + farms
    vm = pl.BlockSpec(memory_space=pltpu.VMEM)
    dma = pltpu.SemaphoreType.DMA
    power, commit, cons = pl.pallas_call(
        functools.partial(kernel, n_tm, n_scen, units),
        name="window",
        out_shape=(
            jax.ShapeDtypeStruct((units, cols), f32),
            jax.ShapeDtypeStruct((units, cols), f32),
            jax.ShapeDtypeStruct((H_DEV, up), f32),
        ),
        in_specs=[vm] * 8 + [pl.BlockSpec(memory_space=pltpu.SMEM)],
        out_specs=(vm,) * 3,
        scratch_shapes=[
            pltpu.VMEM((lines, wide), bf16),
            pltpu.VMEM((up, lines), bf16),
            pltpu.VMEM((lines, cols), f32),
            pltpu.VMEM((lines, cols), f32),
            pltpu.VMEM((lines, cols), bf16),
            pltpu.VMEM((up, cols), f32),
            pltpu.VMEM((up, cols), f32),
            pltpu.VMEM((up, cols), f32),
            pltpu.VMEM((up, cols), f32),
            pltpu.VMEM((wide, cols), bf16),
            pltpu.VMEM((up, cols), f32),
            pltpu.VMEM((up, 128), f32),
            pltpu.VMEM((up, 128), f32),
            pltpu.VMEM((n_scen, H_DEV, rows), bf16),
            pltpu.VMEM((PASSES, 2, up // 4, 128), f32),
            pltpu.VMEM((PASSES, 2, up // 4, 128), f32),
            pltpu.VMEM((H_DEV, up), f32),
            pltpu.VMEM((n_scen, H_DEV, up), f32),
            pltpu.VMEM((1, cols), f32),
            pltpu.VMEM((H_DEV, up), f32),
            pltpu.VMEM((up, H_DEV), f32),
            dma((n_scen * 4,)),
            dma((5, n_scen * 4)),
            dma((n_scen,)),
            dma((n_scen,)),
            dma((PASSES, 2)),
            dma((PASSES, 2)),
            dma((n_scen,)),
            dma((n_scen,)),
        ],
        compiler_params=pltpu.CompilerParams(collective_id=0, has_side_effects=True, vmem_limit_bytes=56 * 1024 * 1024),
    )(sel, load_flows.T, prior_dispatch, prior_commitment, prior_consensus.T, prior_multiplier, wind_output, unit_table, demand)
    steps = 1
    tiles = pl.BlockSpec((units // steps, cols), lambda i: (i, 0))
    power, commit, cons, updated = pl.pallas_call(
        functools.partial(finish, units),
        name="finish",
        out_shape=(
            jax.ShapeDtypeStruct((units, cols), f32),
            jax.ShapeDtypeStruct((units, cols), f32),
            jax.ShapeDtypeStruct((H_DEV, units), f32),
            jax.ShapeDtypeStruct((units, cols), f32),
        ),
        grid=(steps,),
        in_specs=[tiles, tiles, tiles, pl.BlockSpec((H_DEV, up), lambda i: (0, 0))],
        out_specs=(tiles, tiles, pl.BlockSpec((H_DEV, units), lambda i: (0, 0)), tiles),
        scratch_shapes=[pltpu.VMEM((up, 3 * H_DEV), f32)],
    )(power, commit, prior_multiplier, cons)
    return power, commit, cons.T, updated


def passed_along(value, axis, steps):
    count = lax.axis_size(axis)
    first, last = (max(0, -steps), min(count, count - steps))
    return lax.ppermute(value, axis, [(source, source + steps) for source in range(first, last)])


def plain(prior_dispatch, prior_commitment, prior_consensus, prior_multiplier, flow_factors,
          unit_buses, wind_buses, wind_output, demand, load_flows, line_limits, unit_table):
    units, columns = prior_dispatch.shape
    block = columns // H_DEV
    linear, quadratic, capacity, ramp_limit, noload = (unit_table[i][:, None] for i in range(5))
    factors = jnp.dot(flow_factors, selection(unit_buses, wind_buses, flow_factors.shape[1], units, jnp.bfloat16),
                      preferred_element_type=jnp.float32).astype(jnp.bfloat16)
    wind_total = jnp.sum(wind_output.astype(jnp.float32), axis=0)
    needed = jnp.repeat(demand, block)
    target = jnp.repeat(prior_consensus, block, axis=1)
    first_block = lax.axis_index("tm") == 0
    last_block = lax.axis_index("tm") == lax.axis_size("tm") - 1
    power, commit = prior_dispatch, prior_commitment
    factors = lax.all_gather(factors, "scen", axis=0, tiled=True)
    hourly = jnp.repeat(lax.all_gather(load_flows, "scen", axis=0, tiled=True).astype(jnp.float32), block, axis=1)
    limit = lax.all_gather(line_limits, "scen", axis=0, tiled=True).astype(jnp.float32)[:, None]
    for _ in range(PASSES):
        extended = jnp.concatenate([power.astype(jnp.bfloat16), wind_output], axis=0)
        flows = jnp.dot(factors, extended, preferred_element_type=jnp.float32) - hourly
        excess = (flows - jnp.clip(flows, -limit, limit)).astype(jnp.bfloat16)
        back = lax.dot_general(factors[:, :units], excess, (((0,), (0,)), ((), ())), preferred_element_type=jnp.float32)
        before = passed_along(power[:, columns - block:], "tm", 1)
        after = passed_along(power[:, :block], "tm", -1)
        before = jnp.where(first_block, power[:, :block], before)
        after = jnp.where(last_block, power[:, columns - block:], after)
        rate = power - jnp.concatenate([before, power[:, :columns - block]], axis=1)
        coming = jnp.concatenate([power[:, block:], after], axis=1) - power
        over = rate - jnp.clip(rate, -ramp_limit, ramp_limit)
        following = coming - jnp.clip(coming, -ramp_limit, ramp_limit)
        balance = jnp.sum(power, axis=0) + wind_total - needed
        short = jnp.maximum(power - capacity * commit, 0.0)
        grad_power = (linear + 2.0 * quadratic * power + flow_weight * back + ramp_weight * (over - following)
                      + balance_weight * balance + short_weight * short)
        grad_commit = noload - short_weight * capacity * short + prior_multiplier + penalty * (commit - target)
        power, commit = (jnp.clip(power - step_power * grad_power, 0.0, capacity),
                         jnp.clip(commit - step_commit * grad_commit, 0.0, 1.0))
    sums = jnp.sum((commit + prior_multiplier / penalty).reshape(units, H_DEV, block), axis=2)
    totals = lax.psum(sums, "scen")
    consensus = jnp.clip(totals / (block * lax.axis_size("scen")), 0.0, 1.0)
    updated = prior_multiplier + penalty * (commit - jnp.repeat(consensus, block, axis=1))
    return power, commit, consensus, updated


def solution(mesh):
    n_tm, n_scen = mesh.shape["tm"], mesh.shape["scen"]

    def per_device(*args):
        rows, cols = args[4].shape[0], args[0].shape[1]
        fits = (n_tm == 4 and n_scen % 2 == 0 and rows % 64 == 0 and cols == 256
                and args[7].shape[0] % 128 == 0 and args[0].shape[0] % 128 > 0)
        if fits:
            return fused(n_tm, n_scen, *args)
        return plain(*args)

    both_axes = P(None, ("tm", "scen"))
    in_specs = (both_axes, both_axes, P(None, "tm"), both_axes, P("scen", None), P(), P(), both_axes,
                P("tm"), P("scen", "tm"), P("scen"), P())
    out_specs = (both_axes, both_axes, P(None, "tm"), both_axes)
    return jax.shard_map(per_device, mesh=mesh, in_specs=in_specs, out_specs=out_specs, check_vma=False)
```
